1024 devices in a mesh: tok: 128 (over x, y_lo, z), head: 8 (over y_hi, core).
Axes of the slice: x: 4, y: 8 (y_hi: 4, y_lo: 2; y = y_hi * 2 + y_lo), z: 16, core: 2. Of those that a mesh axis runs over, the one named last changes fastest.
Arguments:
- queries_first: bfloat16 [32768, 3072], P('tok', 'head'), may hold values from -180 to 180
- queries_second: bfloat16 [32768, 3072], P('tok', 'head'), may hold values from -180 to 180
- grads_first: bfloat16 [32768, 3072], P('tok', 'head'), may hold values from -6 to 6
- grads_second: bfloat16 [32768, 3072], P('tok', 'head'), may hold values from -6 to 6
- key_states: bfloat16 [32768, 1024], P('tok', 'head'), may hold values from -4.5 to 4.5
- value_states: bfloat16 [32768, 1024], P('tok', 'head'), may hold values from -6 to 6
- doc_lengths: int32 [128], replicated, may hold values from 1 to 768, 32768 in all
- hidden_states: bfloat16 [32768, 3072], P('tok', 'head'), may hold values from -24 to 24
Outputs:
- grad_queries_first: bfloat16 [32768, 3072], P('tok', 'head')
- grad_queries_second: bfloat16 [32768, 3072], P('tok', 'head')
- weight_grad: float32 [3072, 2048], P('tok', 'head')
The draws below stay inside these ranges and needn't reach their ends.
All inputs are finite; a program needn't handle non-finite values.
Results may differ from the reference program's by a relative error of at most 0.0075.
Values may be sent and summed in bfloat16 or wider, within the bound.
A program may use at most 32 MiB of HBM per device.

```python
import math
import jax
import jax.numpy as jnp
import numpy as np
from jax import lax

D = 3072
QH = 24
KVH = 8
HD = 128
TOK_DEV = 256
REACH = 3
SEQ = 32768
DOC_MAX = 768
NDOCS = 128


def shared_keys(key):
    drawn = jnp.clip(jax.random.normal(jax.random.fold_in(key, 101), (SEQ, KVH * HD), jnp.float32), -4.5, 4.5)
    return drawn


def drawn_queries(key, offset):
    entries = jnp.clip(jax.random.normal(jax.random.fold_in(key, offset), (SEQ, QH * HD), jnp.float32), -4.5, 4.5)
    return entries


def draw_key_states(key, part):
    return shared_keys(key).astype(jnp.bfloat16)


def draw_queries_first(key, part):
    return drawn_queries(key, 201).astype(jnp.bfloat16)


def draw_queries_second(key, part):
    return drawn_queries(key, 202).astype(jnp.bfloat16)


def spiked(result, rng, source, target, shards_of, factor):
    def block_of(axis_at):
        return (jnp.arange(result.shape[axis_at]) // (result.shape[axis_at] // shards_of)).reshape((-1,) + (1,) * (result.ndim - 1 - axis_at))

    first = jax.random.permutation(rng, shards_of)[block_of(target)]
    far = (block_of(target) + shards_of // 2) % shards_of
    return jnp.where((block_of(source) == first) | (block_of(source) == far), factor * result, result)


def block_levels(key, dims, cuts, least, largest):
    def one(axis_at, blocks):
        heights = jax.random.uniform(jax.random.fold_in(jax.random.fold_in(key, 6), axis_at), (blocks,), jnp.float32, least / len(cuts), largest / len(cuts))
        return jnp.repeat(jnp.exp(heights), dims[axis_at] // blocks).reshape((-1,) + (1,) * (len(dims) - axis_at - 1))

    level = one(*cuts[0])
    for cut in cuts[1:]:
        level = level * one(*cut)
    return level


def split_up(number_of, total, limit, skew):
    loads = [(1 << 20) // math.isqrt(standing ** skew) + 1 for standing in range(2, number_of + 1)]
    surplus, counts = total - limit - (number_of - 1), [1] * (number_of - 1)
    while surplus > 0:
        candidates = [i for i in range(number_of - 1) if counts[i] < limit]
        whole, budget = sum([loads[i] for i in candidates]), surplus
        for i in candidates:
            more = min(limit - counts[i], max(1, budget * loads[i] // whole), surplus)
            counts[i] = counts[i] + more
            surplus = surplus - more
    return np.array([limit] + counts)


def ragged(key, count, total, limit, slope):
    if count == 2:
        one = jax.random.randint(key, (), max(1, total - limit), min(limit, total - 1) + 1)
        return jnp.stack([one, total - one])
    lengths = jnp.asarray(split_up(count, total, limit, slope), jnp.int32)
    twos = (count - 1) // 2
    source_of, taker = lengths[1:1 + 2 * twos:2], lengths[2:2 + 2 * twos:2]
    slack = jnp.minimum(source_of - 1, limit - taker)
    passed = jax.random.randint(jax.random.fold_in(key, 1), (twos,), 0, 1 << 20) % (slack + 1)
    lengths = lengths.at[1:1 + 2 * twos:2].set(source_of - passed).at[2:2 + 2 * twos:2].set(taker + passed)
    return lengths[jax.random.permutation(jax.random.fold_in(key, 2), count)]


def normal_values(own_key, shape, scale, most, split=(), held_as=jnp.bfloat16):
    entries = scale * jax.random.normal(own_key, shape, jnp.float32)
    if split:
        entries = entries * block_levels(own_key, shape, split, -0.22, 0.18)
    return jnp.clip(entries, -most, most).astype(held_as)


def heavy_noise(key, extent, scale, reach, shards, heavy, held_as=jnp.bfloat16):
    values = scale * jax.random.normal(key, extent, jnp.float32)
    if shards:
        values = values * block_levels(key, extent, shards, -0.22, 0.18)
    return jnp.clip(spiked(values, jax.random.fold_in(key, 3), *heavy), -reach, reach).astype(held_as)


def setup_inputs(seed: int = 0) -> dict:
    splits = jax.random.split(jax.random.key(seed), 9)
    return {
        "queries_first": draw_queries_first(jax.random.fold_in(splits[8], 71), 0),
        "queries_second": draw_queries_second(jax.random.fold_in(splits[8], 71), 0),
        "grads_first": normal_values(splits[2], (SEQ, QH * HD), 1.0, 6.0, ((0, 128), (1, 8))),
        "grads_second": normal_values(splits[3], (SEQ, QH * HD), 1.0, 6.0, ((0, 128), (1, 8))),
        "key_states": draw_key_states(jax.random.fold_in(splits[8], 71), 0),
        "value_states": normal_values(splits[5], (SEQ, KVH * HD), 1.0, 6.0, ((0, 128), (1, 8))),
        "doc_lengths": ragged(splits[6], NDOCS, SEQ, DOC_MAX, 2).astype(jnp.int32),
        "hidden_states": heavy_noise(splits[7], (SEQ, D), 1.0, 24.0, ((0, 128), (1, 8)), (0, 1, 128, 5.5)),
    }


def document_of(places, doc_ends):
    return lax.optimization_barrier(jnp.sum((places[:, None] >= doc_ends[None, :]).astype(jnp.int32), axis=1))

def causal_mask(query_places, key_places, doc_ends):
    same_doc = document_of(query_places, doc_ends)[:, None] == document_of(jnp.maximum(key_places, 0), doc_ends)[None, :]
    return same_doc & (key_places[None, :] <= query_places[:, None]) & (key_places[None, :] >= 0)

def attend_grads(queries, grad_rows, key_window, value_window, allowed):
    query_rows = queries.shape[0]
    window = key_window.shape[0]
    kv_heads = key_window.shape[1] // HD
    group_size = queries.shape[1] // (kv_heads * HD)
    score_scale = 1.0 / math.sqrt(HD)
    q_four = queries.reshape(query_rows, kv_heads, group_size, HD).astype(jnp.float32)
    g_four = grad_rows.reshape(query_rows, kv_heads, group_size, HD).astype(jnp.float32)
    k_three = key_window.reshape(window, kv_heads, HD).astype(jnp.float32)
    v_three = value_window.reshape(window, kv_heads, HD).astype(jnp.float32)
    scores = jnp.einsum('bhgd,whd->hgbw', q_four, k_three) * score_scale
    scores = jnp.where(allowed, scores, -1e+30)
    row_max = lax.optimization_barrier(jnp.max(scores, axis=-1, keepdims=True))
    raised = jnp.exp(scores - row_max)
    prob_rows = raised / lax.optimization_barrier(jnp.sum(raised, axis=-1, keepdims=True))
    prob_half = prob_rows.astype(jnp.bfloat16).astype(jnp.float32)
    outputs = jnp.einsum('hgbw,whd->bhgd', prob_half, v_three)
    deltas = lax.optimization_barrier(jnp.sum(g_four * outputs, axis=-1))
    deltas = jnp.transpose(deltas, (1, 2, 0))[..., None]
    grad_prob = jnp.einsum('bhgd,whd->hgbw', g_four, v_three)
    grad_score = (prob_rows * (grad_prob - deltas)).astype(jnp.bfloat16).astype(jnp.float32)
    grad_query = (jnp.einsum('hgbw,whd->bhgd', grad_score, k_three) * score_scale).astype(jnp.bfloat16)
    grad_key = jnp.einsum('hgbw,bhgd->whd', grad_score, q_four) * score_scale
    grad_value = jnp.einsum('hgbw,bhgd->whd', prob_half, g_four)
    return (grad_query.reshape(query_rows, -1), grad_key, grad_value)

def reference(queries_first, queries_second, grads_first, grads_second, key_states, value_states, doc_lengths, hidden_states):
    padding = REACH * TOK_DEV
    window = (REACH + 1) * TOK_DEV
    kv_width = key_states.shape[1]
    stacked = jnp.concatenate([key_states, value_states], axis=1)
    stacked = jnp.concatenate([jnp.zeros((padding, stacked.shape[1]), stacked.dtype), stacked], axis=0)
    doc_ends = jnp.cumsum(doc_lengths).astype(jnp.int32)
    start_grads = jnp.zeros((SEQ + padding, 2 * kv_width), jnp.float32)

    def one_block(running, block_index):
        start = (block_index * TOK_DEV).astype(jnp.int32)
        window_rows = lax.dynamic_slice_in_dim(stacked, start, window, 0)
        key_window = window_rows[:, :kv_width]
        value_window = window_rows[:, kv_width:]
        query_places = start + jnp.arange(TOK_DEV, dtype=jnp.int32)
        key_places = start - padding + jnp.arange(window, dtype=jnp.int32)
        allowed = causal_mask(query_places, key_places, doc_ends)
        first_q, first_k, first_v = attend_grads(lax.dynamic_slice_in_dim(queries_first, start, TOK_DEV, 0), lax.dynamic_slice_in_dim(grads_first, start, TOK_DEV, 0), key_window, value_window, allowed)
        second_q, second_k, second_v = attend_grads(lax.dynamic_slice_in_dim(queries_second, start, TOK_DEV, 0), lax.dynamic_slice_in_dim(grads_second, start, TOK_DEV, 0), key_window, value_window, allowed)
        window_grads = jnp.stack([first_k + second_k, first_v + second_v], axis=2).reshape(window, -1)
        updated = lax.dynamic_slice_in_dim(running, start, window, 0) + window_grads
        running = lax.dynamic_update_slice_in_dim(running, updated, start, 0)
        return (running, (first_q, second_q))
    running, (all_first, all_second) = lax.scan(one_block, start_grads, jnp.arange(SEQ // TOK_DEV, dtype=jnp.int32))
    kv_grads = running[padding:].astype(jnp.bfloat16)
    weight_grad = jnp.dot(hidden_states.T, kv_grads, preferred_element_type=jnp.float32)
    return (all_first.reshape(SEQ, -1), all_second.reshape(SEQ, -1), weight_grad)
```

```python
import math

import jax
import jax.numpy as jnp
from jax import lax
from jax.sharding import PartitionSpec as P

HD = 128
REACH = 3


def passed_along(value, axis, steps):
    count = lax.axis_size(axis)
    initial, last = (max(0, -steps), min(count, count - steps))
    return lax.ppermute(value, axis, [(source, source + steps) for source in range(initial, last)])


def document_of(places, doc_ends):
    return jnp.sum((places[:, None] >= doc_ends[None, :]).astype(jnp.int32), axis=1)


def causal_mask(query_places, key_places, doc_ends):
    same_doc = (
        document_of(query_places, doc_ends)[:, None]
        == document_of(jnp.maximum(key_places, 0), doc_ends)[None, :]
    )
    return same_doc & (key_places[None, :] <= query_places[:, None]) & (key_places[None, :] >= 0)


def attend_grads(queries, grad_rows, key_window, value_window, allowed):
    query_rows = queries.shape[0]
    window = key_window.shape[0]
    kv_heads = key_window.shape[1] // HD
    group_size = queries.shape[1] // (kv_heads * HD)
    score_scale = 1.0 / math.sqrt(HD)
    q_four = queries.reshape(query_rows, kv_heads, group_size, HD)
    g_four = grad_rows.reshape(query_rows, kv_heads, group_size, HD)
    k_three = key_window.reshape(window, kv_heads, HD)
    v_three = value_window.reshape(window, kv_heads, HD)
    scores = (
        jnp.einsum("bhgd,whd->hgbw", q_four, k_three, preferred_element_type=jnp.float32)
        * score_scale
    )
    scores = jnp.where(allowed, scores, -1e30)
    row_max = jnp.max(scores, axis=-1, keepdims=True)
    raised = jnp.exp(scores - row_max)
    prob_rows = raised / jnp.sum(raised, axis=-1, keepdims=True)
    prob_half = prob_rows.astype(jnp.bfloat16)
    outputs = jnp.einsum("hgbw,whd->bhgd", prob_half, v_three, preferred_element_type=jnp.float32)
    deltas = jnp.sum(g_four.astype(jnp.float32) * outputs, axis=-1)
    deltas = jnp.transpose(deltas, (1, 2, 0))[..., None]
    grad_prob = jnp.einsum("bhgd,whd->hgbw", g_four, v_three, preferred_element_type=jnp.float32)
    grad_score = (prob_rows * (grad_prob - deltas)).astype(jnp.bfloat16)
    grad_query = (
        jnp.einsum("hgbw,whd->bhgd", grad_score, k_three, preferred_element_type=jnp.float32)
        * score_scale
    ).astype(jnp.bfloat16)
    grad_key = (
        jnp.einsum("hgbw,bhgd->whd", grad_score, q_four, preferred_element_type=jnp.float32)
        * score_scale
    )
    grad_value = jnp.einsum("hgbw,bhgd->whd", prob_half, g_four, preferred_element_type=jnp.float32)
    return (grad_query.reshape(query_rows, -1), grad_key, grad_value)


def projection_term(full_rows, grad_part):
    return lax.dot_general(
        full_rows, grad_part, (((0,), (0,)), ((), ())), preferred_element_type=jnp.float32
    )


PARTS = 8
DEPTH = 16
STRIDED = [[part * DEPTH + z for part in range(PARTS)] for z in range(DEPTH)]
RUNS = [[part * DEPTH + z for z in range(DEPTH)] for part in range(PARTS)]
SWAP = [
    ((i * DEPTH + z) * PARTS + j, (j * DEPTH + z) * PARTS + i)
    for i in range(PARTS)
    for z in range(DEPTH)
    for j in range(PARTS)
]


def gathered_hidden(hidden_states):
    column = lax.all_gather(
        hidden_states, "tok", axis=0, tiled=True, axis_index_groups=STRIDED
    )
    return lax.ppermute(column, ("tok", "head"), SWAP)


def body(
    queries_first,
    queries_second,
    grads_first,
    grads_second,
    key_states,
    value_states,
    doc_lengths,
    hidden_states,
):
    tok_rows = key_states.shape[0]
    kv_width = key_states.shape[1]
    window = (REACH + 1) * tok_rows
    here = lax.axis_index("tok")
    stacked = jnp.concatenate([key_states, value_states], axis=1)
    blocks = [stacked]
    current = stacked
    for hop_count in range(REACH):
        current = passed_along(current, "tok", 1)
        blocks.append(current)
    window_rows = jnp.concatenate(blocks[::-1], axis=0)
    key_window = window_rows[:, :kv_width]
    value_window = window_rows[:, kv_width:]
    doc_ends = jnp.cumsum(doc_lengths)
    query_places = here * tok_rows + jnp.arange(tok_rows, dtype=jnp.int32)
    key_places = (here - REACH) * tok_rows + jnp.arange(window, dtype=jnp.int32)
    allowed = causal_mask(query_places, key_places, doc_ends)
    first_q, first_k, first_v = attend_grads(
        queries_first, grads_first, key_window, value_window, allowed
    )
    second_q, second_k, second_v = attend_grads(
        queries_second, grads_second, key_window, value_window, allowed
    )
    window_grads = jnp.stack([first_k + second_k, first_v + second_v], axis=2).reshape(window, -1)

    def block_term(back_steps):
        return window_grads[(REACH - back_steps) * tok_rows : (REACH - back_steps + 1) * tok_rows]

    running = block_term(0)
    for back_steps in range(1, REACH + 1):
        running = running + passed_along(
            block_term(back_steps).astype(jnp.bfloat16), "tok", -back_steps
        ).astype(jnp.float32)
    kv_grads = running.astype(jnp.bfloat16)
    rows_here = gathered_hidden(hidden_states)
    grads_here = lax.all_gather(kv_grads, "tok", axis=0, tiled=True, axis_index_groups=STRIDED)
    weight_grad = lax.psum_scatter(
        projection_term(rows_here, grads_here),
        "tok",
        scatter_dimension=0,
        tiled=True,
        axis_index_groups=RUNS,
    )
    return (first_q, second_q, weight_grad)


def solution(mesh):
    placed = (
        P("tok", "head"),
        P("tok", "head"),
        P("tok", "head"),
        P("tok", "head"),
        P("tok", "head"),
        P("tok", "head"),
        P(),
        P("tok", "head"),
    )
    return jax.shard_map(
        body,
        mesh=mesh,
        in_specs=placed,
        out_specs=(P("tok", "head"), P("tok", "head"), P("tok", "head")),
        check_vma=False,
    )
```

```python
import math

import jax
import jax.numpy as jnp
from jax import lax
from jax.experimental import pallas as pl
from jax.experimental.pallas import tpu as pltpu
from jax.sharding import PartitionSpec as P

HD = 128
ROWS = 256
GROUP = 3
LAYERS = 2
PAIRS = LAYERS * GROUP
WIDTH = GROUP * HD
WINDOW = 4
NX = 4
NYL = 2
NZ = 16
NYH = 4
NCORE = 2
TOKS = NX * NYL * NZ
SLOTS = NX * NYL
OUT_ROWS = WIDTH // NZ
SCALE = 1.0 / math.sqrt(HD)
MASKED = -1e30
MESH = pl.DeviceIdType.MESH
F32 = jnp.float32
BF16 = jnp.bfloat16
FAR_FIRST = sorted(range(1, NZ), key=lambda d: -min(d, NZ - d))


def dot_nt(a, b):
    return lax.dot_general(a, b, (((1,), (1,)), ((), ())), preferred_element_type=F32)


def dot_nn(a, b):
    return lax.dot_general(a, b, (((1,), (0,)), ((), ())), preferred_element_type=F32)


def kernel(
    q1_in, q2_in, g1_in, g2_in, k_in, v_in, hid_in, docs,
    dq1_out, dq2_out, wg_out,
    qv, gv, kvb, e, dp, bias, st_m, st_l, st_d, fac, delta, acck, accv, dqt, dqv,
    gs, gr, s1, a2, a3, at, bb, st, rs,
    in_sem, out_sem, halo_send, halo_recv, grad_send, grad_recv,
    s1_send, s1_recv, s2_send, s2_recv, s3_send, s3_recv,
    b_send, b_recv, rs_send, rs_recv,
):
    t = lax.axis_index("tok")
    h = lax.axis_index("head")
    z = lax.rem(t, NZ)
    i = lax.div(t, NZ)
    yl = lax.rem(i, NYL)
    x = lax.div(i, NYL)
    core = lax.rem(h, NCORE)
    yh = lax.div(h, NCORE)

    def tok_of(xx, yy, zz):
        return (xx * NYL + yy) * NZ + zz

    t_next = lax.rem(t + 1, TOKS)
    t_prev = lax.rem(t + TOKS - 1, TOKS)
    sibling = h + 1 - 2 * core
    y_pair = tok_of(x, 1 - yl, z)

    def x_tok(step):
        return tok_of(lax.rem(x + step, NX), yl, z)

    def z_tok(step):
        return i * NZ + lax.rem(z + step, NZ)

    def fan_id(step):
        return (tok_of(x, core, z), lax.rem(yh + step, NYH) * NCORE + yl)

    crossed = yl != core

    def send(src, dst, send_sem, recv_sem, where):
        return pltpu.make_async_remote_copy(
            src_ref=src, dst_ref=dst, send_sem=send_sem, recv_sem=recv_sem,
            device_id=where, device_id_type=MESH,
        )

    loads = [
        pltpu.make_async_copy(k_in, kvb.at[3, 0], in_sem.at[0]),
        pltpu.make_async_copy(v_in, kvb.at[3, 1], in_sem.at[1]),
        pltpu.make_async_copy(q1_in, qv.at[0], in_sem.at[2]),
        pltpu.make_async_copy(q2_in, qv.at[1], in_sem.at[3]),
        pltpu.make_async_copy(g1_in, gv.at[0], in_sem.at[4]),
        pltpu.make_async_copy(g2_in, gv.at[1], in_sem.at[5]),
    ]
    for load in loads:
        load.start()

    barrier = pltpu.get_barrier_semaphore()

    def greet(where):
        pl.semaphore_signal(barrier, inc=1, device_id=where, device_id_type=MESH)

    for d in FAR_FIRST:
        greet((z_tok(d), h))
    for d in range(1, NYH):
        greet(fan_id(d))

    @pl.when(crossed)
    def _():
        greet(fan_id(0))

    for d in range(1, NX):
        greet((x_tok(d), h))
    greet((y_pair, h))
    greet((t_next, h))
    greet((t_prev, h))
    greet((t, sibling))

    lengths = docs[...].astype(F32)
    row = lax.broadcasted_iota(jnp.int32, (128, 128), 0)
    col = lax.broadcasted_iota(jnp.int32, (128, 128), 1)
    ends = jnp.sum(jnp.where(col <= row, lengths, 0.0), axis=1, keepdims=True)
    base = (t * ROWS).astype(F32)
    place = base + lax.broadcasted_iota(jnp.int32, (128, ROWS), 1).astype(F32)
    first = jnp.max(jnp.where(ends <= place, ends, 0.0), axis=0, keepdims=True)
    first = (first - base).astype(jnp.int32) + (WINDOW - 1) * ROWS

    pl.semaphore_wait(barrier, 15 + 3 + 3 + 1 + 2 + 1 + lax.rem(yl + core, 2))

    def halo(hop, s):
        src = (k_in, v_in)[s] if hop == 0 else kvb.at[3 - hop, s]
        return send(
            src, kvb.at[2 - hop, s], halo_send.at[hop, s], halo_recv.at[hop, s], (t_next, h)
        )

    def fan(step):
        return send(hid_in, s1.at[step], s1_send.at[step], s1_recv.at[step], fan_id(step))

    halo(0, 0).start()
    halo(0, 1).start()
    for d in (2, 1, 3):
        fan(d).start()

    @pl.when(crossed)
    def _():
        fan(0).start()

    @pl.when(jnp.logical_not(crossed))
    def _():
        pltpu.make_async_copy(hid_in, s1.at[0], s1_recv.at[0]).start()

    for load in loads:
        load.wait()

    key_row = lax.broadcasted_iota(jnp.int32, (ROWS, ROWS), 0)
    query_col = lax.broadcasted_iota(jnp.int32, (ROWS, ROWS), 1)

    def scores_of(b):
        seen = key_row + b * ROWS >= first
        if b == WINDOW - 1:
            seen = seen & (key_row <= query_col)
        bias[...] = jnp.where(seen, 0.0, MASKED)

        def one_head(g, carry):
            cols = pl.ds(pl.multiple_of(g * HD, HD), HD)
            for layer in range(LAYERS):
                pair = layer * GROUP + g
                s = dot_nt(kvb[b, 0], qv[layer, :, cols]) * SCALE + bias[...]
                top = jnp.max(s, axis=0, keepdims=True)
                raised = jnp.exp(s - top)
                grad = dot_nt(kvb[b, 1], gv[layer, :, cols])
                e[b, pair] = raised
                dp[b, pair] = grad
                st_m[b, pair] = top
                st_l[b, pair] = jnp.sum(raised, axis=0, keepdims=True)
                st_d[b, pair] = jnp.sum(raised * grad, axis=0, keepdims=True)
            return carry

        lax.fori_loop(0, GROUP, one_head, 0)

    scores_of(3)
    for hop in range(2):
        for s in range(2):
            halo(hop, s).wait_recv()
            halo(hop + 1, s).start()
        scores_of(2 - hop)
    for s in range(2):
        halo(2, s).wait_recv()
    scores_of(0)

    for pair in range(PAIRS):
        top = st_m[0, pair]
        for b in range(1, WINDOW):
            top = jnp.maximum(top, st_m[b, pair])
        weights = [jnp.exp(st_m[b, pair] - top) for b in range(WINDOW)]
        total = weights[0] * st_l[0, pair]
        moved = weights[0] * st_d[0, pair]
        for b in range(1, WINDOW):
            total = total + weights[b] * st_l[b, pair]
            moved = moved + weights[b] * st_d[b, pair]
        inverse = 1.0 / total
        delta[pair] = moved * inverse
        for b in range(WINDOW):
            fac[b, pair] = weights[b] * inverse

    def grads_of(b):
        keys_t = jnp.transpose(kvb[b, 0])
        accv[...] = jnp.zeros_like(accv)
        acck[...] = jnp.zeros_like(acck)

        def one_head(g, carry):
            cols = pl.ds(pl.multiple_of(g * HD, HD), HD)
            for layer in range(LAYERS):
                pair = layer * GROUP + g
                probs = e[b, pair] * fac[b, pair]
                shift = (probs * (dp[b, pair] - delta[pair])).astype(BF16)
                accv[...] += dot_nn(probs.astype(BF16), gv[layer, :, cols])
                acck[...] += dot_nn(shift, qv[layer, :, cols])
                term = dot_nn(keys_t, shift)
                if b == 0:
                    dqt[pair] = term
                else:
                    dqt[pair] += term
            return carry

        lax.fori_loop(0, GROUP, one_head, 0)

    def pass_back(b, s):
        return send(
            gs.at[b, s], gr.at[b, s], grad_send.at[b, s], grad_recv.at[b, s], (t_prev, h)
        )

    def hand_over(b, s):
        mine = accv[...] if s == 1 else acck[...] * SCALE
        if b > 0:
            pass_back(b - 1, s).wait_recv()
            mine = mine + gr[b - 1, s].astype(F32)
        if b < WINDOW - 1:
            gs[b, s] = mine.astype(BF16)
            pass_back(b, s).start()
        else:
            bb[s, 0] = mine.astype(BF16)

    def column_slot(step):
        return lax.rem(yh + 2 * NX - x - step, NX)

    def across(step):
        return send(
            s1.at[column_slot(step)], a2.at[step], s2_send.at[step], s2_recv.at[step],
            (x_tok(step), h),
        )

    def own_block(step):
        return s1.at[column_slot(0)] if step == 0 else a2.at[step]

    def share(step):
        return send(
            own_block(step), a3.at[step], s3_send.at[step], s3_recv.at[step], (t, sibling)
        )

    grads_of(0)
    hand_over(0, 1)
    hand_over(0, 0)
    grads_of(1)
    hand_over(1, 1)
    hand_over(1, 0)
    for step in (2, 1, 3, 0):
        slot = column_slot(step)
        send(
            hid_in, s1.at[slot], s1_send.at[slot], s1_recv.at[slot], (t_next, h)
        ).wait_recv()
        if step:
            across(step).start()
    grads_of(2)
    hand_over(2, 1)
    hand_over(2, 0)
    grads_of(3)

    for pair in range(PAIRS):
        layer, g = divmod(pair, GROUP)
        dqv[layer, :, g * HD : (g + 1) * HD] = (jnp.transpose(dqt[pair]) * SCALE).astype(BF16)
    stores = [
        pltpu.make_async_copy(dqv.at[0], dq1_out, out_sem.at[0]),
        pltpu.make_async_copy(dqv.at[1], dq2_out, out_sem.at[1]),
    ]
    for store in stores:
        store.start()

    def spread(s, src, dst, where):
        return send(
            bb.at[s, src], bb.at[s, dst], b_send.at[s, dst], b_recv.at[s, dst], (where, h)
        )

    def from_pair(s):
        return spread(s, 0, 1, y_pair)

    def own_up(s):
        return spread(s, 0, 2, x_tok(1))

    def own_down(s):
        return spread(s, 0, 6, x_tok(3))

    def pair_up(s):
        return spread(s, 1, 3, x_tok(1))

    def pair_down(s):
        return spread(s, 1, 7, x_tok(3))

    def own_far(s):
        return spread(s, 2, 4, x_tok(1))

    def pair_far(s):
        return spread(s, 7, 5, x_tok(3))

    for s in (1, 0):
        hand_over(3, s)
        from_pair(s).start()
        own_up(s).start()
        own_down(s).start()

    share(0).start()
    for step in range(1, NX):
        across(step).wait_recv()
        share(step).start()

    for s in (1, 0):
        from_pair(s).wait_recv()
        pair_down(s).start()
        pair_up(s).start()
        own_up(s).wait_recv()
        own_far(s).start()

    def slot_of(step, dy):
        return step * NYL + dy

    near = lax.rem(yl + core, 2)
    at[near] = jnp.transpose(s1[column_slot(0)])
    for step in range(1, NX):
        at[slot_of(step, near)] = jnp.transpose(a2[step])

    for s in (1, 0):
        pair_down(s).wait_recv()
        pair_far(s).start()

    for step in range(NX):
        share(step).wait_recv()
        at[slot_of(step, 1 - near)] = jnp.transpose(a3[step])

    def scatter(s, step):
        return send(
            st.at[s, lax.rem(z + step, NZ)], rs.at[s, step], rs_send.at[s, step],
            rs_recv.at[s, step], (z_tok(step), h),
        )

    for s in (1, 0):
        for landed in (own_down, pair_up, own_far, pair_far):
            landed(s).wait_recv()
        total = dot_nn(at[0], bb[s, 0])
        for slot in range(1, SLOTS):
            total = total + dot_nn(at[slot], bb[s, slot])
        st[s] = total.reshape(NZ, OUT_ROWS, HD).astype(BF16)
        for step in FAR_FIRST:
            scatter(s, step).start()

    for s in (1, 0):
        summed = st[s, z].astype(F32)
        for step in range(1, NZ):
            scatter(s, step).wait_recv()
            summed = summed + rs[s, step].astype(F32)
        wg_out[:, s * HD : (s + 1) * HD] = summed

    for store in stores:
        store.wait()
    for hop in range(3):
        for s in range(2):
            halo(hop, s).wait_send()
            pass_back(hop, s).wait_send()
    for step in range(1, NYH):
        fan(step).wait_send()

    @pl.when(crossed)
    def _():
        fan(0).wait_send()

    for step in range(NX):
        if step:
            across(step).wait_send()
        share(step).wait_send()
    for s in range(2):
        for sent in (from_pair, own_up, own_down, pair_up, pair_down, own_far, pair_far):
            sent(s).wait_send()
        for step in range(1, NZ):
            scatter(s, step).wait_send()


def body(
    queries_first,
    queries_second,
    grads_first,
    grads_second,
    key_states,
    value_states,
    doc_lengths,
    hidden_states,
):
    anywhere = pl.BlockSpec(memory_space=pl.ANY)
    in_vmem = pl.BlockSpec(memory_space=pltpu.VMEM)
    dma = pltpu.SemaphoreType.DMA
    vmem = pltpu.VMEM
    return pl.pallas_call(
        kernel,
        out_shape=(
            jax.ShapeDtypeStruct((ROWS, WIDTH), BF16),
            jax.ShapeDtypeStruct((ROWS, WIDTH), BF16),
            jax.ShapeDtypeStruct((OUT_ROWS, 2 * HD), F32),
        ),
        in_specs=[anywhere] * 7 + [in_vmem],
        out_specs=(anywhere, anywhere, in_vmem),
        scratch_shapes=[
            vmem((LAYERS, ROWS, WIDTH), BF16),
            vmem((LAYERS, ROWS, WIDTH), BF16),
            vmem((WINDOW, 2, ROWS, HD), BF16),
            vmem((WINDOW, PAIRS, ROWS, ROWS), F32),
            vmem((WINDOW, PAIRS, ROWS, ROWS), F32),
            vmem((ROWS, ROWS), F32),
            vmem((WINDOW, PAIRS, 1, ROWS), F32),
            vmem((WINDOW, PAIRS, 1, ROWS), F32),
            vmem((WINDOW, PAIRS, 1, ROWS), F32),
            vmem((WINDOW, PAIRS, 1, ROWS), F32),
            vmem((PAIRS, 1, ROWS), F32),
            vmem((ROWS, HD), F32),
            vmem((ROWS, HD), F32),
            vmem((PAIRS, HD, ROWS), F32),
            vmem((LAYERS, ROWS, WIDTH), BF16),
            vmem((WINDOW - 1, 2, ROWS, HD), BF16),
            vmem((WINDOW - 1, 2, ROWS, HD), BF16),
            vmem((NYH, ROWS, WIDTH), BF16),
            vmem((NX, ROWS, WIDTH), BF16),
            vmem((NX, ROWS, WIDTH), BF16),
            vmem((SLOTS, WIDTH, ROWS), BF16),
            vmem((2, SLOTS, ROWS, HD), BF16),
            vmem((2, NZ, OUT_ROWS, HD), BF16),
            vmem((2, NZ, OUT_ROWS, HD), BF16),
            dma((6,)), dma((2,)), dma((3, 2)), dma((3, 2)), dma((3, 2)), dma((3, 2)),
            dma((NYH,)), dma((NYH,)), dma((NX,)), dma((NX,)), dma((NX,)), dma((NX,)),
            dma((2, SLOTS)), dma((2, SLOTS)), dma((2, NZ)), dma((2, NZ)),
        ],
        compiler_params=pltpu.CompilerParams(
            collective_id=0, has_side_effects=True, vmem_limit_bytes=48 << 20
        ),
    )(
        queries_first,
        queries_second,
        grads_first,
        grads_second,
        key_states,
        value_states,
        hidden_states,
        doc_lengths.reshape(1, 128),
    )


def solution(mesh):
    spread = P("tok", "head")
    return jax.shard_map(
        body,
        mesh=mesh,
        in_specs=(spread,) * 6 + (P(), spread),
        out_specs=(spread, spread, spread),
        check_vma=False,
    )
```

```python
import math

import jax
import jax.numpy as jnp
from jax import lax
from jax.experimental import pallas as pl
from jax.experimental.pallas import tpu as pltpu
from jax.sharding import PartitionSpec as P

HD = 128
ROWS = 256
GROUP = 3
LAYERS = 2
PAIRS = LAYERS * GROUP
WIDTH = GROUP * HD
WINDOW = 4
NX = 4
NYL = 2
NZ = 16
NYH = 4
NCORE = 2
TOKS = NX * NYL * NZ
SLOTS = NX * NYL
OUT_ROWS = WIDTH // NZ
SCALE = 1.0 / math.sqrt(HD)
MASKED = -1e30
MESH = pl.DeviceIdType.MESH
F32 = jnp.float32
BF16 = jnp.bfloat16
FAR_FIRST = sorted(range(1, NZ), key=lambda d: -min(d, NZ - d))


def dot_nt(a, b):
    return lax.dot_general(a, b, (((1,), (1,)), ((), ())), preferred_element_type=F32)


def dot_nn(a, b):
    return lax.dot_general(a, b, (((1,), (0,)), ((), ())), preferred_element_type=F32)


def kernel(
    q1_in, q2_in, g1_in, g2_in, k_in, v_in, hid_in, docs,
    dq1_out, dq2_out, wg_out,
    qv, gv, kvb, e, dp, bias, st_m, st_l, st_d, fac, delta, acck, accv, dqt, dqv,
    gs, gr, s1, a2, a3, at, bb, st, rs,
    in_sem, out_sem, halo_send, halo_recv, grad_send, grad_recv,
    s1_send, s1_recv, relay_send, s2_send, s2_recv, s3_send, s3_recv,
    b_send, b_recv, rs_send, rs_recv,
):
    t = lax.axis_index("tok")
    h = lax.axis_index("head")
    z = lax.rem(t, NZ)
    i = lax.div(t, NZ)
    yl = lax.rem(i, NYL)
    x = lax.div(i, NYL)
    core = lax.rem(h, NCORE)
    yh = lax.div(h, NCORE)

    def tok_of(xx, yy, zz):
        return (xx * NYL + yy) * NZ + zz

    t_next = lax.rem(t + 1, TOKS)
    t_prev = lax.rem(t + TOKS - 1, TOKS)
    sibling = h + 1 - 2 * core
    y_pair = tok_of(x, 1 - yl, z)

    def x_tok(step):
        return tok_of(lax.rem(x + step, NX), yl, z)

    def z_tok(step):
        return i * NZ + lax.rem(z + step, NZ)

    def fan_id(step):
        return (tok_of(x, core, z), lax.rem(yh + step, NYH) * NCORE + yl)

    case_same_low = jnp.logical_and(yl == 0, core == 0)
    case_same_high = jnp.logical_and(yl == 1, core == 1)
    case_low_high = jnp.logical_and(yl == 0, core == 1)
    case_high_low = jnp.logical_and(yl == 1, core == 0)
    crossed = yl != core

    def head_at(step):
        return lax.rem(yh + step, NYH) * NCORE + core

    def send(src, dst, send_sem, recv_sem, where):
        return pltpu.make_async_remote_copy(
            src_ref=src, dst_ref=dst, send_sem=send_sem, recv_sem=recv_sem,
            device_id=where, device_id_type=MESH,
        )

    loads = [
        pltpu.make_async_copy(k_in, kvb.at[3, 0], in_sem.at[0]),
        pltpu.make_async_copy(v_in, kvb.at[3, 1], in_sem.at[1]),
        pltpu.make_async_copy(q1_in, qv.at[0], in_sem.at[2]),
        pltpu.make_async_copy(q2_in, qv.at[1], in_sem.at[3]),
        pltpu.make_async_copy(g1_in, gv.at[0], in_sem.at[4]),
        pltpu.make_async_copy(g2_in, gv.at[1], in_sem.at[5]),
    ]
    for load in loads:
        load.start()

    barrier = pltpu.get_barrier_semaphore()

    def greet(where):
        pl.semaphore_signal(barrier, inc=1, device_id=where, device_id_type=MESH)

    for d in FAR_FIRST:
        greet((z_tok(d), h))
    for d in range(1, NYH):
        greet(fan_id(d))

    @pl.when(crossed)
    def _():
        greet(fan_id(0))

    for d in range(1, NX):
        greet((x_tok(d), h))
    greet((y_pair, h))
    greet((t_next, h))
    greet((t_prev, h))
    greet((t, sibling))
    greet((t, head_at(1)))
    greet((t, head_at(NYH - 1)))

    lengths = docs[...].astype(F32)
    row = lax.broadcasted_iota(jnp.int32, (128, 128), 0)
    col = lax.broadcasted_iota(jnp.int32, (128, 128), 1)
    ends = jnp.sum(jnp.where(col <= row, lengths, 0.0), axis=1, keepdims=True)
    base = (t * ROWS).astype(F32)
    place = base + lax.broadcasted_iota(jnp.int32, (128, ROWS), 1).astype(F32)
    first = jnp.max(jnp.where(ends <= place, ends, 0.0), axis=0, keepdims=True)
    first = (first - base).astype(jnp.int32) + (WINDOW - 1) * ROWS

    pl.semaphore_wait(barrier, 15 + 3 + 3 + 1 + 2 + 1 + 2 + lax.rem(yl + core, 2))

    def halo(hop, s):
        src = (k_in, v_in)[s] if hop == 0 else kvb.at[3 - hop, s]
        return send(
            src, kvb.at[2 - hop, s], halo_send.at[hop, s], halo_recv.at[hop, s], (t_next, h)
        )

    def fan(step):
        return send(hid_in, s1.at[step], s1_send.at[step], s1_recv.at[step], fan_id(step))

    halo(0, 0).start()
    halo(0, 1).start()
    def sends(act):
        @pl.when(jnp.logical_not(crossed))
        def _():
            act(1)
            act(3)

        @pl.when(case_low_high)
        def _():
            act(0)
            act(3)

        @pl.when(case_high_low)
        def _():
            act(0)
            act(1)

    sends(lambda step: fan(step).start())

    @pl.when(jnp.logical_not(crossed))
    def _():
        pltpu.make_async_copy(hid_in, s1.at[0], s1_recv.at[0]).start()

    for load in loads:
        load.wait()

    key_row = lax.broadcasted_iota(jnp.int32, (ROWS, ROWS), 0)
    query_col = lax.broadcasted_iota(jnp.int32, (ROWS, ROWS), 1)

    def scores_of(b):
        seen = key_row + b * ROWS >= first
        if b == WINDOW - 1:
            seen = seen & (key_row <= query_col)
        bias[...] = jnp.where(seen, 0.0, MASKED)

        def one_head(g, carry):
            cols = pl.ds(pl.multiple_of(g * HD, HD), HD)
            for layer in range(LAYERS):
                pair = layer * GROUP + g
                s = dot_nt(kvb[b, 0], qv[layer, :, cols]) * SCALE + bias[...]
                top = jnp.max(s, axis=0, keepdims=True)
                raised = jnp.exp(s - top)
                grad = dot_nt(kvb[b, 1], gv[layer, :, cols])
                e[b, pair] = raised
                dp[b, pair] = grad
                st_m[b, pair] = top
                st_l[b, pair] = jnp.sum(raised, axis=0, keepdims=True)
                st_d[b, pair] = jnp.sum(raised * grad, axis=0, keepdims=True)
            return carry

        lax.fori_loop(0, GROUP, one_head, 0)

    scores_of(3)
    for hop in range(2):
        for s in range(2):
            halo(hop, s).wait_recv()
            halo(hop + 1, s).start()
        scores_of(2 - hop)
    for s in range(2):
        halo(2, s).wait_recv()
    def column_slot(step):
        return lax.rem(yh + 2 * NX - x - step, NX)

    def across(step):
        return send(
            s1.at[column_slot(step)], a2.at[step], s2_send.at[step], s2_recv.at[step],
            (x_tok(step), h),
        )

    def landed_at(slot):
        send(
            hid_in, s1.at[slot], s1_send.at[slot], s1_recv.at[slot], (t_next, h)
        ).wait_recv()

    def relay(slot, step):
        after = (slot + step) % NYH
        return send(
            s1.at[slot], s1.at[after], relay_send.at[after], s1_recv.at[after],
            (t, head_at(step)),
        )

    def move_on(slot):
        step = lax.rem(yh + 2 * NX - x - slot, NX)

        @pl.when(step > 0)
        def _():
            send(
                s1.at[slot], a2.at[step], s2_send.at[step], s2_recv.at[step], (x_tok(step), h)
            ).start()

        @pl.when(step == 0)
        def _():
            share(0).start()

    def first_blocks(act):
        @pl.when(case_same_low)
        def _():
            act(((1, 1), (3, 0), (0, 0)))

        @pl.when(case_same_high)
        def _():
            act(((3, 3), (1, 0), (0, 0)))

        @pl.when(case_high_low)
        def _():
            act(((0, 1), (3, 3)))

        @pl.when(case_low_high)
        def _():
            act(((1, 1), (0, 3)))

    def take_first(blocks):
        for slot, step in blocks:
            landed_at(slot)
            if step:
                relay(slot, step).start()
        for slot, step in blocks:
            move_on(slot)

    def take_second():
        def take(slot):
            landed_at(slot)
            move_on(slot)

        @pl.when(jnp.logical_not(crossed))
        def _():
            take(2)

        @pl.when(case_high_low)
        def _():
            take(1)
            take(2)

        @pl.when(case_low_high)
        def _():
            take(2)
            take(3)

    def own_block(step):
        return s1.at[column_slot(0)] if step == 0 else a2.at[step]

    def share(step):
        return send(
            own_block(step), a3.at[step], s3_send.at[step], s3_recv.at[step], (t, sibling)
        )

    scores_of(0)
    first_blocks(take_first)

    for pair in range(PAIRS):
        top = st_m[0, pair]
        for b in range(1, WINDOW):
            top = jnp.maximum(top, st_m[b, pair])
        weights = [jnp.exp(st_m[b, pair] - top) for b in range(WINDOW)]
        total = weights[0] * st_l[0, pair]
        moved = weights[0] * st_d[0, pair]
        for b in range(1, WINDOW):
            total = total + weights[b] * st_l[b, pair]
            moved = moved + weights[b] * st_d[b, pair]
        inverse = 1.0 / total
        delta[pair] = moved * inverse
        for b in range(WINDOW):
            fac[b, pair] = weights[b] * inverse

    def grads_of(b):
        keys_t = jnp.transpose(kvb[b, 0])
        accv[...] = jnp.zeros_like(accv)
        acck[...] = jnp.zeros_like(acck)

        def one_head(g, carry):
            cols = pl.ds(pl.multiple_of(g * HD, HD), HD)
            for layer in range(LAYERS):
                pair = layer * GROUP + g
                probs = e[b, pair] * fac[b, pair]
                shift = (probs * (dp[b, pair] - delta[pair])).astype(BF16)
                accv[...] += dot_nn(probs.astype(BF16), gv[layer, :, cols])
                acck[...] += dot_nn(shift, qv[layer, :, cols])
                term = dot_nn(keys_t, shift)
                if b == 0:
                    dqt[pair] = term
                else:
                    dqt[pair] += term
            return carry

        lax.fori_loop(0, GROUP, one_head, 0)

    def pass_back(b, s):
        return send(
            gs.at[b, s], gr.at[b, s], grad_send.at[b, s], grad_recv.at[b, s], (t_prev, h)
        )

    def hand_over(b, s):
        mine = accv[...] if s == 1 else acck[...] * SCALE
        if b > 0:
            pass_back(b - 1, s).wait_recv()
            mine = mine + gr[b - 1, s].astype(F32)
        if b < WINDOW - 1:
            gs[b, s] = mine.astype(BF16)
            pass_back(b, s).start()
        else:
            bb[s, 0] = mine.astype(BF16)

    grads_of(0)
    hand_over(0, 1)
    hand_over(0, 0)
    grads_of(1)
    hand_over(1, 1)
    hand_over(1, 0)
    take_second()
    grads_of(2)
    hand_over(2, 1)
    hand_over(2, 0)
    grads_of(3)

    for pair in range(PAIRS):
        layer, g = divmod(pair, GROUP)
        dqv[layer, :, g * HD : (g + 1) * HD] = (jnp.transpose(dqt[pair]) * SCALE).astype(BF16)
    stores = [
        pltpu.make_async_copy(dqv.at[0], dq1_out, out_sem.at[0]),
        pltpu.make_async_copy(dqv.at[1], dq2_out, out_sem.at[1]),
    ]
    for store in stores:
        store.start()

    def spread(s, src, dst, where):
        return send(
            bb.at[s, src], bb.at[s, dst], b_send.at[s, dst], b_recv.at[s, dst], (where, h)
        )

    def from_pair(s):
        return spread(s, 0, 1, y_pair)

    def own_up(s):
        return spread(s, 0, 2, x_tok(1))

    def own_down(s):
        return spread(s, 0, 6, x_tok(3))

    def pair_up(s):
        return spread(s, 1, 3, x_tok(1))

    def pair_down(s):
        return spread(s, 1, 7, x_tok(3))

    def own_far(s):
        return spread(s, 2, 4, x_tok(1))

    def pair_far(s):
        return spread(s, 7, 5, x_tok(3))

    for s in (1, 0):
        hand_over(3, s)
        from_pair(s).start()
        own_up(s).start()
        own_down(s).start()

    def slot_of(step, dy):
        return step * NYL + dy

    near = lax.rem(yl + core, 2)
    for step in range(1, NX):
        across(step).wait_recv()
        share(step).start()
    at[near] = jnp.transpose(s1[column_slot(0)])
    for step in range(1, NX):
        at[slot_of(step, near)] = jnp.transpose(a2[step])

    for s in (1, 0):
        from_pair(s).wait_recv()
        pair_down(s).start()
        pair_up(s).start()
        own_up(s).wait_recv()
        own_far(s).start()

    for step in range(NX):
        share(step).wait_recv()
        at[slot_of(step, 1 - near)] = jnp.transpose(a3[step])

    for s in (1, 0):
        pair_down(s).wait_recv()
        pair_far(s).start()

    def scatter(s, step):
        return send(
            st.at[s, lax.rem(z + step, NZ)], rs.at[s, step], rs_send.at[s, step],
            rs_recv.at[s, step], (z_tok(step), h),
        )

    for s in (1, 0):
        for landed in (own_down, pair_up, own_far, pair_far):
            landed(s).wait_recv()
        total = dot_nn(at[0], bb[s, 0])
        for slot in range(1, SLOTS):
            total = total + dot_nn(at[slot], bb[s, slot])
        st[s] = total.reshape(NZ, OUT_ROWS, HD).astype(BF16)
        for step in FAR_FIRST:
            scatter(s, step).start()

    for s in (1, 0):
        summed = st[s, z].astype(F32)
        for step in range(1, NZ):
            scatter(s, step).wait_recv()
            summed = summed + rs[s, step].astype(F32)
        wg_out[:, s * HD : (s + 1) * HD] = summed

    for store in stores:
        store.wait()
    for hop in range(3):
        for s in range(2):
            halo(hop, s).wait_send()
            pass_back(hop, s).wait_send()
    sends(lambda step: fan(step).wait_send())

    def relays_left(blocks):
        for slot, step in blocks:
            if step:
                relay(slot, step).wait_send()

    first_blocks(relays_left)
    for step in range(NX):
        if step:
            across(step).wait_send()
        share(step).wait_send()
    for s in range(2):
        for sent in (from_pair, own_up, own_down, pair_up, pair_down, own_far, pair_far):
            sent(s).wait_send()
        for step in range(1, NZ):
            scatter(s, step).wait_send()


def body(
    queries_first,
    queries_second,
    grads_first,
    grads_second,
    key_states,
    value_states,
    doc_lengths,
    hidden_states,
):
    anywhere = pl.BlockSpec(memory_space=pl.ANY)
    in_vmem = pl.BlockSpec(memory_space=pltpu.VMEM)
    dma = pltpu.SemaphoreType.DMA
    vmem = pltpu.VMEM
    return pl.pallas_call(
        kernel,
        out_shape=(
            jax.ShapeDtypeStruct((ROWS, WIDTH), BF16),
            jax.ShapeDtypeStruct((ROWS, WIDTH), BF16),
            jax.ShapeDtypeStruct((OUT_ROWS, 2 * HD), F32),
        ),
        in_specs=[anywhere] * 7 + [in_vmem],
        out_specs=(anywhere, anywhere, in_vmem),
        scratch_shapes=[
            vmem((LAYERS, ROWS, WIDTH), BF16),
            vmem((LAYERS, ROWS, WIDTH), BF16),
            vmem((WINDOW, 2, ROWS, HD), BF16),
            vmem((WINDOW, PAIRS, ROWS, ROWS), F32),
            vmem((WINDOW, PAIRS, ROWS, ROWS), F32),
            vmem((ROWS, ROWS), F32),
            vmem((WINDOW, PAIRS, 1, ROWS), F32),
            vmem((WINDOW, PAIRS, 1, ROWS), F32),
            vmem((WINDOW, PAIRS, 1, ROWS), F32),
            vmem((WINDOW, PAIRS, 1, ROWS), F32),
            vmem((PAIRS, 1, ROWS), F32),
            vmem((ROWS, HD), F32),
            vmem((ROWS, HD), F32),
            vmem((PAIRS, HD, ROWS), F32),
            vmem((LAYERS, ROWS, WIDTH), BF16),
            vmem((WINDOW - 1, 2, ROWS, HD), BF16),
            vmem((WINDOW - 1, 2, ROWS, HD), BF16),
            vmem((NYH, ROWS, WIDTH), BF16),
            vmem((NX, ROWS, WIDTH), BF16),
            vmem((NX, ROWS, WIDTH), BF16),
            vmem((SLOTS, WIDTH, ROWS), BF16),
            vmem((2, SLOTS, ROWS, HD), BF16),
            vmem((2, NZ, OUT_ROWS, HD), BF16),
            vmem((2, NZ, OUT_ROWS, HD), BF16),
            dma((6,)), dma((2,)), dma((3, 2)), dma((3, 2)), dma((3, 2)), dma((3, 2)),
            dma((NYH,)), dma((NYH,)), dma((NYH,)), dma((NX,)), dma((NX,)), dma((NX,)), dma((NX,)),
            dma((2, SLOTS)), dma((2, SLOTS)), dma((2, NZ)), dma((2, NZ)),
        ],
        compiler_params=pltpu.CompilerParams(
            collective_id=0, has_side_effects=True, vmem_limit_bytes=67043328
        ),
    )(
        queries_first,
        queries_second,
        grads_first,
        grads_second,
        key_states,
        value_states,
        hidden_states,
        doc_lengths.reshape(1, 128),
    )


def solution(mesh):
    spread = P("tok", "head")
    return jax.shard_map(
        body,
        mesh=mesh,
        in_specs=(spread,) * 6 + (P(), spread),
        out_specs=(spread, spread, spread),
        check_vma=False,
    )
```
